128 devices in a mesh: nodes: 32 (over x, z, core), feat: 4 (over y).
Axes of the slice: x: 4, y: 4, z: 4, core: 2. Of those that a mesh axis runs over, the one named last changes fastest.
Arguments:
- features: bfloat16 [262144, 256], P('nodes', 'feat'), may hold values from -6 to 6
- weight: bfloat16 [256, 256], P(None, 'feat'), may hold values from -0.375 to 0.375
- adj_tiles: bfloat16 [12288, 128, 128], P('nodes'), may hold values from -0.21875 to 0.21875
- tile_row: int32 [12288], P('nodes'), may hold values from 0 to 63, as said below
- tile_col: int32 [12288], P('nodes'), may hold values from 0 to 2047, as said below
- cotangent: bfloat16 [262144, 256], P('nodes', 'feat'), may hold values from -6 to 6
Outputs:
- activated: bfloat16 [262144, 256], P('nodes', 'feat')
- grad_features: bfloat16 [262144, 256], P('nodes', 'feat')
- grad_weight: float32 [256, 256], P(None, 'feat')
The draws below stay inside these ranges and needn't reach their ends.
Inputs may be any that keep to these rules, and one draw needn't show every extreme that they name: `tile_row`: tile k * 384 + s with s < 64 has block row s. Every device has at least one tile in each of its block rows. `tile_col`: tile k * 384 + s with s < 64 has column block k * 64 + s, the diagonal tile. Of a device's tiles, at most 2 have their column block on any one other device, and exactly 2 on its successor (k + 1) mod 32.
All inputs are finite; a program needn't handle non-finite values.
Results may differ from the reference program's by a relative error of at most 0.0061.
Values may be sent and summed in bfloat16 or wider, within the bound.
A program may use at most 192 MiB of HBM per device.

```python
import math
import jax
import jax.numpy as jnp
from jax import lax

F = 256
BLK = 128
K = 6
CAP = 2
B_DEV = 64
S_DEV = 384
NB = 2048
NODES = 262144
SLOTS = 12288
N_NODES = 32


def build_graph(key):
    peers_count = NB // B_DEV
    slot_count = B_DEV * K
    base = jax.random.fold_in(key, 4177)
    key_counts, key_blocks, key_rows = jax.random.split(base, 3)
    device_ids = jnp.arange(peers_count, dtype=jnp.int32)[:, None]
    peer_ids = jnp.arange(peers_count, dtype=jnp.int32)[None, :]
    counts = jax.random.randint(key_counts, (peers_count, peers_count), 0, CAP + 1).astype(jnp.int32)
    counts = jnp.where(peer_ids == device_ids, 0, counts)
    counts = jnp.where(peer_ids == (device_ids + 1) % peers_count, CAP, counts)
    ends = jnp.cumsum(counts, axis=1).astype(jnp.int32)
    slot_ids = jnp.arange(slot_count, dtype=jnp.int32)[None, :]
    offset = slot_ids - B_DEV
    owner_found = jnp.sum((ends[:, None, :] <= offset[:, :, None]).astype(jnp.int32), axis=2)
    remote = (offset >= 0) & (offset < ends[:, -1:])
    owners = jnp.where(remote, owner_found, device_ids)
    within = jax.random.randint(key_blocks, (peers_count, slot_count), 0, B_DEV).astype(jnp.int32)
    diagonal = slot_ids < B_DEV
    blocks = jnp.where(diagonal, slot_ids % B_DEV, within)
    cols = (owners * B_DEV + blocks).astype(jnp.int32)
    random_rows = jax.random.randint(key_rows, (peers_count, slot_count), 0, B_DEV).astype(jnp.int32)
    rows = jnp.where(diagonal, slot_ids % B_DEV, random_rows).astype(jnp.int32)
    return (rows.reshape(-1), cols.reshape(-1))


def draw_tile_row(key, part):
    return build_graph(key)[0]


def draw_tile_col(key, part):
    return build_graph(key)[1]


def shard_levels(rng, dims, shards, smallest, largest):
    factor_of, own = 1.0, jax.random.fold_in(rng, 6)
    for dim, parts in shards:
        draws = jnp.exp(jax.random.uniform(jax.random.fold_in(own, dim), (parts,), jnp.float32, smallest / len(shards), largest / len(shards)))
        factor_of = factor_of * jnp.repeat(draws, dims[dim] // parts).reshape([-1 if axis == dim else 1 for axis in range(len(dims))])
    return factor_of


def noise(stream_key, shape, deviation, limit, cuts=(), held_as=jnp.bfloat16):
    result = deviation * jax.random.normal(stream_key, shape, jnp.float32)
    if cuts:
        result = result * shard_levels(stream_key, shape, cuts, -0.22, 0.18)
    return jnp.clip(result, -limit, limit).astype(held_as)


def setup_inputs(seed: int = 0) -> dict:
    keys = jax.random.split(jax.random.key(seed), 7)
    features = noise(keys[0], (NODES, F), 1.0, 6.0, ((0, 32), (1, 4)))
    weight = noise(keys[1], (F, F), F ** -0.5, 0.375, ((1, 4),))
    adj_tiles = noise(keys[2], (SLOTS, BLK, BLK), (BLK * K) ** -0.5, 0.21875, ((0, 32),))
    tile_row = draw_tile_row(jax.random.fold_in(keys[6], 71), 0)
    tile_col = draw_tile_col(jax.random.fold_in(keys[6], 71), 0)
    cotangent = noise(keys[5], (NODES, F), 1.0, 6.0, ((0, 32), (1, 4)))
    return dict(features=features, weight=weight, adj_tiles=adj_tiles, tile_row=tile_row, tile_col=tile_col, cotangent=cotangent)


def reference(features, weight, adj_tiles, tile_row, tile_col, cotangent):
    highest = lax.Precision.HIGHEST
    proj = jnp.dot(features, weight, preferred_element_type=jnp.float32).astype(jnp.bfloat16)
    proj_blocks = proj.reshape(NB, BLK, F).astype(jnp.float32)
    block_ids = jnp.arange(B_DEV, dtype=jnp.int32)
    devices = jnp.arange(N_NODES, dtype=jnp.int32)

    def forward_one(device):
        start = (device * S_DEV).astype(jnp.int32)
        tiles_here = lax.dynamic_slice_in_dim(adj_tiles, start, S_DEV, 0).astype(jnp.float32)
        rows_here = lax.dynamic_slice_in_dim(tile_row, start, S_DEV, 0)
        cols_here = lax.dynamic_slice_in_dim(tile_col, start, S_DEV, 0)
        partials = jnp.einsum('sij,sjf->sif', tiles_here, proj_blocks[cols_here], precision=highest)
        onehot = (rows_here[:, None] == block_ids[None, :]).astype(jnp.float32)
        return jnp.einsum('sr,sif->rif', onehot, partials, precision=highest)
    pre_act = lax.map(forward_one, devices).reshape(NODES, F)
    activated = jax.nn.silu(pre_act).astype(jnp.bfloat16)
    sigmoid_vals = jax.nn.sigmoid(pre_act)
    grad_pre = (cotangent.astype(jnp.float32) * sigmoid_vals * (1.0 + pre_act * (1.0 - sigmoid_vals))).astype(jnp.bfloat16)
    grad_blocks = grad_pre.reshape(NB, BLK, F).astype(jnp.float32)

    def backward_one(total, device):
        start = (device * S_DEV).astype(jnp.int32)
        tiles_here = lax.dynamic_slice_in_dim(adj_tiles, start, S_DEV, 0).astype(jnp.float32)
        rows_here = lax.dynamic_slice_in_dim(tile_row, start, S_DEV, 0)
        cols_here = lax.dynamic_slice_in_dim(tile_col, start, S_DEV, 0)
        global_rows = (device * B_DEV + rows_here).astype(jnp.int32)
        back_terms = jnp.einsum('sji,sjf->sif', tiles_here, grad_blocks[global_rows], precision=highest)
        return (total.at[cols_here].add(back_terms), None)
    grad_total, unused = lax.scan(backward_one, jnp.zeros((NB, BLK, F), jnp.float32), devices)
    grad_proj = grad_total.reshape(NODES, F).astype(jnp.bfloat16)
    grad_features = jnp.dot(grad_proj, weight.T, preferred_element_type=jnp.float32).astype(jnp.bfloat16)
    grad_weight = jnp.dot(features.T, grad_proj, preferred_element_type=jnp.float32) / math.sqrt(NODES)
    return (activated, grad_features, grad_weight)
```

```python
import functools
import math

import jax
import jax.numpy as jnp
from jax import lax
from jax.experimental import pallas as pl
from jax.experimental.pallas import tpu as pltpu
from jax.sharding import PartitionSpec as P

CAP = 2
STEP = 32
VMEM = pltpu.MemorySpace.VMEM
NT = (((1,), (1,)), ((), ()))
NN = (((1,), (0,)), ((), ()))


def whole():
    return pl.BlockSpec(memory_space=VMEM)


def params():
    return pltpu.CompilerParams(vmem_limit_bytes=48 * 1024 * 1024)


def proj_kernel(ids, wt_ref, x_ref, proj_ref, send_ref):
    step = pl.program_id(0)
    made = jnp.dot(wt_ref[...], x_ref[...], preferred_element_type=jnp.float32)
    made = made.astype(jnp.bfloat16)
    per_step = x_ref.shape[1] // 128
    for b in range(per_step):
        proj_ref[step * per_step + b] = made[:, b * 128 : (b + 1) * 128]

    @pl.when(step == pl.num_programs(0) - 1)
    def _():
        @pl.loop(0, send_ref.shape[0], unroll=4)
        def _(e):
            send_ref[e] = proj_ref[ids[e]]


def project(ids, wt, full_t, blocks):
    width, depth = wt.shape
    nodes = full_t.shape[1]
    chunk = 1024
    entries = ids.shape[0]
    return pl.pallas_call(
        proj_kernel,
        grid_spec=pltpu.PrefetchScalarGridSpec(
            num_scalar_prefetch=1,
            grid=(nodes // chunk,),
            in_specs=[
                pl.BlockSpec((width, depth), lambda i, ids: (0, 0)),
                pl.BlockSpec((depth, chunk), lambda i, ids: (0, i)),
            ],
            out_specs=[
                pl.BlockSpec((blocks, width, 128), lambda i, ids: (0, 0, 0)),
                pl.BlockSpec((entries, width, 128), lambda i, ids: (0, 0, 0)),
            ],
        ),
        out_shape=[
            jax.ShapeDtypeStruct((blocks, width, 128), jnp.bfloat16),
            jax.ShapeDtypeStruct((entries, width, 128), jnp.bfloat16),
        ],
        compiler_params=params(),
        cost_estimate=pl.CostEstimate(
            flops=2 * nodes * depth * width, bytes_accessed=12 << 20, transcendentals=0
        ),
        name="project",
    )(ids, wt, full_t)


def tile_kernel(dims, src, dst, x_ref, tile_ref, acc_ref, part_ref):
    step = pl.program_id(0)

    @pl.when(step == 0)
    def _():
        acc_ref[...] = jnp.zeros_like(acc_ref)

    base = step * STEP
    for t in range(STEP):
        part_ref[t] = lax.dot_general(
            x_ref[src[base + t]], tile_ref[t], dims, preferred_element_type=jnp.float32
        )
    for t in range(STEP):
        acc_ref[dst[base + t]] += part_ref[t]


def local_tiles(dims, src, dst, x, tiles, name):
    blocks, width, size = x.shape
    count = tiles.shape[0]
    return pl.pallas_call(
        functools.partial(tile_kernel, dims),
        grid_spec=pltpu.PrefetchScalarGridSpec(
            num_scalar_prefetch=2,
            grid=(count // STEP,),
            in_specs=[
                pl.BlockSpec((blocks, width, size), lambda i, s, d: (0, 0, 0)),
                pl.BlockSpec((STEP, size, size), lambda i, s, d: (i, 0, 0)),
            ],
            out_specs=pl.BlockSpec((blocks + 1, width, size), lambda i, s, d: (0, 0, 0)),
            scratch_shapes=[pltpu.VMEM((STEP, width, size), jnp.float32)],
        ),
        out_shape=jax.ShapeDtypeStruct((blocks + 1, width, size), jnp.float32),
        compiler_params=params(),
        cost_estimate=pl.CostEstimate(
            flops=8 * count * size * size * width, bytes_accessed=20 << 20, transcendentals=0
        ),
        name=name,
    )(src, dst, x, tiles)


def middle_kernel(
    slots, rows, acc_ref, recv_ref, cot_ref, tiles_ref, act_ref, grad_ref, send_ref,
    held, extra, grads, part, sems,
):
    entries = recv_ref.shape[0]
    blocks = grad_ref.shape[0]

    @pl.loop(0, entries)
    def _(e):
        pltpu.make_async_copy(tiles_ref.at[slots[e]], held.at[e], sems.at[e]).start()

    extra[...] = jnp.zeros_like(extra)
    grads[blocks] = jnp.zeros_like(grads[blocks])

    @pl.loop(0, entries)
    def _(e):
        pltpu.make_async_copy(tiles_ref.at[slots[e]], held.at[e], sems.at[e]).wait()

    @pl.loop(0, entries // 16)
    def _(g):
        for t in range(16):
            part[t] = lax.dot_general(
                recv_ref[g * 16 + t], held[g * 16 + t], NT, preferred_element_type=jnp.float32
            )
        for t in range(16):
            extra[rows[g * 16 + t]] += part[t]

    @pl.loop(0, blocks, unroll=2)
    def _(b):
        cols = pl.ds(pl.multiple_of(b * 128, 128), 128)
        v = acc_ref[b] + extra[b]
        s = jax.nn.sigmoid(v)
        act_ref[:, cols] = (v * s).astype(jnp.bfloat16)
        grad = cot_ref[:, cols].astype(jnp.float32) * s * (1.0 + v * (1.0 - s))
        grad = grad.astype(jnp.bfloat16)
        grads[b] = grad
        grad_ref[b] = grad

    @pl.loop(0, entries // 16)
    def _(g):
        for t in range(16):
            send_ref[g * 16 + t] = lax.dot_general(
                grads[rows[g * 16 + t]], held[g * 16 + t], NN,
                preferred_element_type=jnp.float32,
            ).astype(jnp.bfloat16)


def middle(slots, rows, acc, recv, cot_t, tiles):
    entries, width, size = recv.shape
    blocks = acc.shape[0] - 1
    nodes = cot_t.shape[1]
    return pl.pallas_call(
        middle_kernel,
        grid_spec=pltpu.PrefetchScalarGridSpec(
            num_scalar_prefetch=2,
            grid=(),
            in_specs=[whole(), whole(), whole(), pl.BlockSpec(memory_space=pl.ANY)],
            out_specs=[whole(), whole(), whole()],
            scratch_shapes=[
                pltpu.VMEM((entries, size, size), jnp.bfloat16),
                pltpu.VMEM((blocks + 1, width, size), jnp.float32),
                pltpu.VMEM((blocks + 1, width, size), jnp.bfloat16),
                pltpu.VMEM((16, width, size), jnp.float32),
                pltpu.SemaphoreType.DMA((entries,)),
            ],
        ),
        out_shape=[
            jax.ShapeDtypeStruct((width, nodes), jnp.bfloat16),
            jax.ShapeDtypeStruct((blocks, width, size), jnp.bfloat16),
            jax.ShapeDtypeStruct((entries, width, size), jnp.bfloat16),
        ],
        compiler_params=params(),
        name="middle",
    )(slots, rows, acc, recv, cot_t, tiles)


def finish_kernel(ids, acc_ref, recv_ref, out_ref, extra):
    extra[...] = jnp.zeros_like(extra)

    @pl.loop(0, recv_ref.shape[0], unroll=4)
    def _(e):
        extra[ids[e]] += recv_ref[e].astype(jnp.float32)

    @pl.loop(0, extra.shape[0], unroll=4)
    def _(b):
        cols = pl.ds(pl.multiple_of(b * 128, 128), 128)
        out_ref[:, cols] = (acc_ref[b] + extra[b]).astype(jnp.bfloat16)


def finish(ids, acc, recv):
    entries, width, size = recv.shape
    blocks = acc.shape[0] - 1
    return pl.pallas_call(
        finish_kernel,
        grid_spec=pltpu.PrefetchScalarGridSpec(
            num_scalar_prefetch=1,
            grid=(),
            in_specs=[whole(), whole()],
            out_specs=whole(),
            scratch_shapes=[pltpu.VMEM((blocks, width, size), jnp.float32)],
        ),
        out_shape=jax.ShapeDtypeStruct((width, blocks * size), jnp.bfloat16),
        compiler_params=params(),
        name="finish",
    )(ids, acc, recv)


def per_device(features, weight, adj_tiles, tile_row, tile_col, cotangent):
    block_size = adj_tiles.shape[1]
    node_rows = features.shape[0]
    blocks = node_rows // block_size
    width = features.shape[1]
    slot_count = adj_tiles.shape[0]
    node_count = lax.axis_size("nodes")
    own = lax.axis_index("nodes")
    feat_index = lax.axis_index("feat")

    owners = tile_col // blocks
    local_block = tile_col - owners * blocks
    slot_ids = jnp.arange(slot_count, dtype=jnp.int32)
    peers = jnp.arange(node_count, dtype=jnp.int32)
    member = (owners[None, :] == peers[:, None]) & (peers[:, None] != own)
    first = jnp.min(jnp.where(member, slot_ids[None, :], slot_count), axis=1)
    last = jnp.max(jnp.where(member, slot_ids[None, :], -1), axis=1)
    found = jnp.stack([first, last], axis=1)
    live = jnp.stack([last >= 0, last > first], axis=1)
    slots = jnp.where(live, found, 0).reshape(-1)
    live = live.reshape(-1)
    hit = slots[:, None] == slot_ids[None, :]
    slot_rows = jnp.sum(jnp.where(hit, tile_row[None, :], 0), axis=1)
    slot_blocks = jnp.sum(jnp.where(hit, local_block[None, :], 0), axis=1)
    rows = jnp.where(live, slot_rows, blocks).astype(jnp.int32)
    asked = jnp.where(live, slot_blocks, 0).astype(jnp.int32)
    every_asked = lax.all_gather(asked, "nodes", axis=0, tiled=False)
    ids = lax.dynamic_slice_in_dim(every_asked, own * CAP, CAP, 1).reshape(-1)

    is_local = owners == own
    src_fwd = jnp.where(is_local, local_block, 0)
    dst_fwd = jnp.where(is_local, tile_row, blocks)
    dst_bwd = jnp.where(is_local, local_block, blocks)

    wt = weight.T
    full_t = lax.all_gather(features.T, "feat", axis=0, tiled=True)
    full_wt = lax.all_gather(wt, "feat", axis=0, tiled=True)
    weight_part = lax.dynamic_slice_in_dim(full_wt, feat_index * width, width, 1)

    proj, send = project(ids, wt, full_t, blocks)
    recv = lax.all_to_all(send, "nodes", split_axis=0, concat_axis=0, tiled=True)
    acc = local_tiles(NT, src_fwd, dst_fwd, proj, adj_tiles, "forward_local")
    act_t, grads, send_back = middle(slots, rows, acc, recv, cotangent.T, adj_tiles)
    recv_back = lax.all_to_all(send_back, "nodes", split_axis=0, concat_axis=0, tiled=True)
    back = local_tiles(NN, tile_row, dst_bwd, grads, adj_tiles, "backward_local")
    gp_t = finish(ids, back, recv_back)
    gp_full = lax.all_gather(gp_t, "feat", axis=0, tiled=True)
    term = jnp.einsum("fn,kn->fk", gp_t, full_t, preferred_element_type=jnp.float32)
    grad_weight = lax.psum(term, "nodes") / math.sqrt(node_rows * node_count)
    gf_t = jnp.einsum("fk,fn->kn", weight_part, gp_full, preferred_element_type=jnp.float32)
    return (act_t.T, gf_t.astype(jnp.bfloat16).T, grad_weight.T)


def solution(mesh):
    return jax.shard_map(
        per_device,
        mesh=mesh,
        in_specs=(
            P("nodes", "feat"),
            P(None, "feat"),
            P("nodes", None, None),
            P("nodes"),
            P("nodes"),
            P("nodes", "feat"),
        ),
        out_specs=(P("nodes", "feat"), P("nodes", "feat"), P(None, "feat")),
        check_vma=False,
    )
```

```python
import functools
import math

import jax
import jax.numpy as jnp
from jax import lax
from jax.experimental import pallas as pl
from jax.experimental.pallas import tpu as pltpu
from jax.sharding import PartitionSpec as P

CAP = 2
STEP = 32
VMEM = pltpu.MemorySpace.VMEM
NT = (((1,), (1,)), ((), ()))
NN = (((1,), (0,)), ((), ()))


def whole():
    return pl.BlockSpec(memory_space=VMEM)


def params():
    return pltpu.CompilerParams(vmem_limit_bytes=48 * 1024 * 1024)


def proj_kernel(ids, wt_ref, x_ref, proj_ref, send_ref):
    step = pl.program_id(0)
    made = jnp.dot(wt_ref[...], x_ref[...], preferred_element_type=jnp.float32)
    made = made.astype(jnp.bfloat16)
    per_step = x_ref.shape[1] // 128
    for b in range(per_step):
        proj_ref[step * per_step + b] = made[:, b * 128 : (b + 1) * 128]

    @pl.when(step == pl.num_programs(0) - 1)
    def _():
        @pl.loop(0, send_ref.shape[0], unroll=4)
        def _(e):
            send_ref[e] = proj_ref[ids[e]]


def project(ids, wt, full_t, blocks):
    width, depth = wt.shape
    nodes = full_t.shape[1]
    chunk = 1024
    entries = ids.shape[0]
    return pl.pallas_call(
        proj_kernel,
        grid_spec=pltpu.PrefetchScalarGridSpec(
            num_scalar_prefetch=1,
            grid=(nodes // chunk,),
            in_specs=[
                pl.BlockSpec((width, depth), lambda i, ids: (0, 0)),
                pl.BlockSpec((depth, chunk), lambda i, ids: (0, i)),
            ],
            out_specs=[
                pl.BlockSpec((blocks, width, 128), lambda i, ids: (0, 0, 0)),
                pl.BlockSpec((entries, width, 128), lambda i, ids: (0, 0, 0)),
            ],
        ),
        out_shape=[
            jax.ShapeDtypeStruct((blocks, width, 128), jnp.bfloat16),
            jax.ShapeDtypeStruct((entries, width, 128), jnp.bfloat16),
        ],
        compiler_params=params(),
        cost_estimate=pl.CostEstimate(
            flops=2 * nodes * depth * width, bytes_accessed=12 << 20, transcendentals=0
        ),
        name="project",
    )(ids, wt, full_t)


def tile_kernel(dims, src, dst, x_ref, tile_ref, acc_ref, part_ref):
    step = pl.program_id(0)

    @pl.when(step == 0)
    def _():
        acc_ref[...] = jnp.zeros_like(acc_ref)

    base = step * STEP
    for t in range(STEP):
        part_ref[t] = lax.dot_general(
            x_ref[src[base + t]], tile_ref[t], dims, preferred_element_type=jnp.float32
        )
    for t in range(STEP):
        acc_ref[dst[base + t]] += part_ref[t]


def local_tiles(dims, src, dst, x, tiles, name):
    blocks, width, size = x.shape
    count = tiles.shape[0]
    return pl.pallas_call(
        functools.partial(tile_kernel, dims),
        grid_spec=pltpu.PrefetchScalarGridSpec(
            num_scalar_prefetch=2,
            grid=(count // STEP,),
            in_specs=[
                pl.BlockSpec((blocks, width, size), lambda i, s, d: (0, 0, 0)),
                pl.BlockSpec((STEP, size, size), lambda i, s, d: (i, 0, 0)),
            ],
            out_specs=pl.BlockSpec((blocks + 1, width, size), lambda i, s, d: (0, 0, 0)),
            scratch_shapes=[pltpu.VMEM((STEP, width, size), jnp.float32)],
        ),
        out_shape=jax.ShapeDtypeStruct((blocks + 1, width, size), jnp.float32),
        compiler_params=params(),
        cost_estimate=pl.CostEstimate(
            flops=8 * count * size * size * width, bytes_accessed=20 << 20, transcendentals=0
        ),
        name=name,
    )(src, dst, x, tiles)


def middle_kernel(
    slots, rows, acc_ref, recv_ref, cot_ref, tiles_ref, act_ref, grad_ref, send_ref,
    held, extra, grads, part, sems,
):
    entries = recv_ref.shape[0]
    blocks = grad_ref.shape[0]

    @pl.loop(0, entries)
    def _(e):
        pltpu.make_async_copy(tiles_ref.at[slots[e]], held.at[e], sems.at[e]).start()

    extra[...] = jnp.zeros_like(extra)
    grads[blocks] = jnp.zeros_like(grads[blocks])

    @pl.loop(0, entries)
    def _(e):
        pltpu.make_async_copy(tiles_ref.at[slots[e]], held.at[e], sems.at[e]).wait()

    @pl.loop(0, entries // 16)
    def _(g):
        for t in range(16):
            part[t] = lax.dot_general(
                recv_ref[g * 16 + t], held[g * 16 + t], NT, preferred_element_type=jnp.float32
            )
        for t in range(16):
            extra[rows[g * 16 + t]] += part[t]

    @pl.loop(0, blocks, unroll=2)
    def _(b):
        cols = pl.ds(pl.multiple_of(b * 128, 128), 128)
        v = acc_ref[b] + extra[b]
        s = jax.nn.sigmoid(v)
        act_ref[:, cols] = (v * s).astype(jnp.bfloat16)
        grad = cot_ref[:, cols].astype(jnp.float32) * s * (1.0 + v * (1.0 - s))
        grad = grad.astype(jnp.bfloat16)
        grads[b] = grad
        grad_ref[b] = grad

    @pl.loop(0, entries // 16)
    def _(g):
        for t in range(16):
            send_ref[g * 16 + t] = lax.dot_general(
                grads[rows[g * 16 + t]], held[g * 16 + t], NN,
                preferred_element_type=jnp.float32,
            ).astype(jnp.bfloat16)


def middle(slots, rows, acc, recv, cot_t, tiles):
    entries, width, size = recv.shape
    blocks = acc.shape[0] - 1
    nodes = cot_t.shape[1]
    return pl.pallas_call(
        middle_kernel,
        grid_spec=pltpu.PrefetchScalarGridSpec(
            num_scalar_prefetch=2,
            grid=(),
            in_specs=[whole(), whole(), whole(), pl.BlockSpec(memory_space=pl.ANY)],
            out_specs=[whole(), whole(), whole()],
            scratch_shapes=[
                pltpu.VMEM((entries, size, size), jnp.bfloat16),
                pltpu.VMEM((blocks + 1, width, size), jnp.float32),
                pltpu.VMEM((blocks + 1, width, size), jnp.bfloat16),
                pltpu.VMEM((16, width, size), jnp.float32),
                pltpu.SemaphoreType.DMA((entries,)),
            ],
        ),
        out_shape=[
            jax.ShapeDtypeStruct((width, nodes), jnp.bfloat16),
            jax.ShapeDtypeStruct((blocks, width, size), jnp.bfloat16),
            jax.ShapeDtypeStruct((entries, width, size), jnp.bfloat16),
        ],
        compiler_params=params(),
        name="middle",
    )(slots, rows, acc, recv, cot_t, tiles)


def finish_kernel(ids, acc_ref, recv_ref, out_ref, extra):
    extra[...] = jnp.zeros_like(extra)

    @pl.loop(0, recv_ref.shape[0], unroll=4)
    def _(e):
        extra[ids[e]] += recv_ref[e].astype(jnp.float32)

    @pl.loop(0, extra.shape[0], unroll=4)
    def _(b):
        cols = pl.ds(pl.multiple_of(b * 128, 128), 128)
        out_ref[:, cols] = (acc_ref[b] + extra[b]).astype(jnp.bfloat16)


def finish(ids, acc, recv):
    entries, width, size = recv.shape
    blocks = acc.shape[0] - 1
    return pl.pallas_call(
        finish_kernel,
        grid_spec=pltpu.PrefetchScalarGridSpec(
            num_scalar_prefetch=1,
            grid=(),
            in_specs=[whole(), whole()],
            out_specs=whole(),
            scratch_shapes=[pltpu.VMEM((blocks, width, size), jnp.float32)],
        ),
        out_shape=jax.ShapeDtypeStruct((width, blocks * size), jnp.bfloat16),
        compiler_params=params(),
        name="finish",
    )(ids, acc, recv)


def per_device(features, weight, adj_tiles, tile_row, tile_col, cotangent):
    block_size = adj_tiles.shape[1]
    node_rows = features.shape[0]
    blocks = node_rows // block_size
    width = features.shape[1]
    slot_count = adj_tiles.shape[0]
    node_count = lax.axis_size("nodes")
    own = lax.axis_index("nodes")
    feat_index = lax.axis_index("feat")

    owners = tile_col // blocks
    local_block = tile_col - owners * blocks
    slot_ids = jnp.arange(slot_count, dtype=jnp.int32)
    peers = jnp.arange(node_count, dtype=jnp.int32)
    member = (owners[None, :] == peers[:, None]) & (peers[:, None] != own)
    first = jnp.min(jnp.where(member, slot_ids[None, :], slot_count), axis=1)
    last = jnp.max(jnp.where(member, slot_ids[None, :], -1), axis=1)
    found = jnp.stack([first, last], axis=1)
    live = jnp.stack([last >= 0, last > first], axis=1)
    slots = jnp.where(live, found, 0).reshape(-1)
    live = live.reshape(-1)
    hit = slots[:, None] == slot_ids[None, :]
    slot_rows = jnp.sum(jnp.where(hit, tile_row[None, :], 0), axis=1)
    slot_blocks = jnp.sum(jnp.where(hit, local_block[None, :], 0), axis=1)
    rows = jnp.where(live, slot_rows, blocks).astype(jnp.int32)
    asked = jnp.where(live, slot_blocks, 0).astype(jnp.int32)
    every_asked = lax.all_gather(asked, "nodes", axis=0, tiled=False)
    ids = lax.dynamic_slice_in_dim(every_asked, own * CAP, CAP, 1).reshape(-1)

    is_local = owners == own
    src_fwd = jnp.where(is_local, local_block, 0)
    dst_fwd = jnp.where(is_local, tile_row, blocks)
    dst_bwd = jnp.where(is_local, local_block, blocks)

    wt = weight.T
    full_t = lax.all_gather(features.T, "feat", axis=0, tiled=True)
    full_wt = lax.all_gather(wt, "feat", axis=0, tiled=True)
    weight_part = lax.dynamic_slice_in_dim(full_wt, feat_index * width, width, 1)

    wt, weight_part = lax.optimization_barrier((wt, weight_part))
    proj, send = project(ids, wt, full_t, blocks)
    recv = lax.all_to_all(send, "nodes", split_axis=0, concat_axis=0, tiled=True)
    acc = local_tiles(NT, src_fwd, dst_fwd, proj, adj_tiles, "forward_local")
    act_t, grads, send_back = middle(slots, rows, acc, recv, cotangent.T, adj_tiles)
    recv_back = lax.all_to_all(send_back, "nodes", split_axis=0, concat_axis=0, tiled=True)
    back = local_tiles(NN, tile_row, dst_bwd, grads, adj_tiles, "backward_local")
    gp_t = finish(ids, back, recv_back)
    gp_full = lax.all_gather(gp_t, "feat", axis=0, tiled=True)
    term = jnp.einsum("fn,kn->fk", gp_t, full_t, preferred_element_type=jnp.float32)
    pieces = term.reshape(node_count, -1, 128)
    pieces = lax.all_to_all(pieces, "nodes", split_axis=0, concat_axis=0, tiled=True)
    piece = jnp.sum(pieces, axis=0) / math.sqrt(node_rows * node_count)
    grad_weight = lax.all_gather(piece, "nodes", axis=0, tiled=True).reshape(term.shape)
    gf_t = jnp.einsum("fk,fn->kn", weight_part, gp_full, preferred_element_type=jnp.float32)
    return (act_t.T, gf_t.astype(jnp.bfloat16).T, grad_weight.T)


def solution(mesh):
    return jax.shard_map(
        per_device,
        mesh=mesh,
        in_specs=(
            P("nodes", "feat"),
            P(None, "feat"),
            P("nodes", None, None),
            P("nodes"),
            P("nodes"),
            P("nodes", "feat"),
        ),
        out_specs=(P("nodes", "feat"), P("nodes", "feat"), P(None, "feat")),
        check_vma=False,
    )
```
